32 devices in a mesh: group: 4 (over z), expert: 8 (over y, x, core).
Axes of the slice: x: 2, y: 2, z: 4, core: 2. Of those that a mesh axis runs over, the one named last changes fastest.
Arguments:
- hidden_in: bfloat16 [4096, 1024], P(('group', 'expert')), parts along dimension 0, may hold values from -6 to 6
- out_grad: bfloat16 [4096, 1024], P(('group', 'expert')), parts along dimension 0, may hold values from -6 to 6
- gate_probs: float32 [4096, 2], P(('group', 'expert')), parts along dimension 0, may hold values from 0.25 to 2
- expert_ids: int32 [4096, 2], P(('group', 'expert')), parts along dimension 0, may hold values from 0 to 31, as said below
- w_gate: bfloat16 [32, 1024, 768], P('expert'), may hold values from -0.1875 to 0.1875
- w_up: bfloat16 [32, 1024, 768], P('expert'), may hold values from -0.1875 to 0.1875
- w_down: bfloat16 [32, 768, 1024], P('expert'), may hold values from -0.0546875 to 0.0546875
Outputs:
- input_grad: bfloat16 [4096, 1024], P(('group', 'expert')), parts along dimension 0
- prob_grad: bfloat16 [4096, 2], P(('group', 'expert')), parts along dimension 0
The draws below stay inside these ranges and needn't reach their ends.
There are 4 independent parts, one for each index of `group`. The reference program is written for one: setup_inputs(seed, part) draws one part's arguments, and reference() takes and returns one part's arrays. A program takes and returns all parts, laid end to end along the dimension named above; an argument that names none is the same for every part. Nothing has to cross between parts.
Inputs may be any that keep to these rules, and one draw needn't show every extreme that they name: `expert_ids`: each row names 2 different experts. Among the 128 rows of one device no expert is named more than 16 times, and in every draw one expert is named exactly 16 times by the rows of every device.
All inputs are finite; a program needn't handle non-finite values.
Results may differ from the reference program's by a relative error of at most 0.0057.
Values may be sent and summed in bfloat16 or wider, within the bound.
No kernel may reach another device: no remote copies, remote signals or barrier semaphores. Data moves between devices by JAX's collectives and lax.ppermute only.
A program may use at most 64 MiB of HBM per device.

```python
import math
import jax
import jax.numpy as jnp
from jax import lax

D = 1024
FF = 768
EXPERTS = 32
TOPK = 2
TOK_DEV = 128
MOST = 16
TOKENS = 1024
N_EXPERT = 8


def draw_expert_ids(key, part):
    hot_key, rest_key = jax.random.split(jax.random.fold_in(key, 7))
    hot_expert = jax.random.randint(hot_key, (), 0, EXPERTS)
    expert_range = jnp.arange(EXPERTS, dtype=jnp.int32)
    offset = 1 << 28

    def one_block(block_key):
        order_key, noise_key = jax.random.split(block_key)
        order = jax.random.permutation(order_key, TOK_DEV)
        forced = order < MOST
        noise = jax.random.randint(noise_key, (TOK_DEV, EXPERTS), 0, 1 << 20)
        scores = noise * EXPERTS + expert_range[None, :]

        def choose(counts, inputs):
            row_scores, is_forced = inputs
            is_hot = expert_range == hot_expert
            blocked = jnp.logical_or(counts >= MOST, is_hot)
            picked = jnp.where(blocked, row_scores - offset, row_scores)
            picked = jnp.where(jnp.logical_and(is_hot, is_forced), row_scores + offset, picked)
            unused, chosen = lax.top_k(picked, TOPK)
            added = jnp.sum((chosen[:, None] == expert_range[None, :]).astype(jnp.int32), axis=0)
            return (counts + added, chosen.astype(jnp.int32))
        unused_counts, chosen_rows = lax.scan(choose, jnp.zeros((EXPERTS,), jnp.int32), (scores, forced))
        return chosen_rows
    block_keys = jax.random.split(rest_key, TOKENS // TOK_DEV)
    return jax.vmap(one_block)(block_keys).reshape(TOKENS, TOPK).astype(jnp.int32)


def level_of(key, dims, shards, low, high):
    gain, own = 1.0, jax.random.fold_in(key, 6)
    for axis_at, parts in shards:
        steps = jnp.exp(jax.random.uniform(jax.random.fold_in(own, axis_at), (parts,), jnp.float32, low / len(shards), high / len(shards)))
        gain = gain * jnp.repeat(steps, dims[axis_at] // parts).reshape([-1 if axis == axis_at else 1 for axis in range(len(dims))])
    return gain


def bell_draw(rng, dims, deviation, limit, cuts=(), kind=jnp.bfloat16):
    factor_of = level_of(rng, dims, cuts, -0.22, 0.18) if cuts else 1.0
    array = jax.random.normal(rng, dims, jnp.float32) * deviation * factor_of
    return jnp.minimum(jnp.maximum(array, -limit), limit).astype(kind)


def setup_inputs(seed: int = 0, part: int = 0) -> dict:
    keys = jax.random.split(jax.random.key(seed), 8)
    part_keys = jax.random.split(jax.random.fold_in(keys[7], part), 8)
    hidden_in = bell_draw(part_keys[0], (TOKENS, D), 1.0, 6.0, ((0, 8),))
    out_grad = bell_draw(part_keys[1], (TOKENS, D), 1.0, 6.0, ((0, 8),))
    gate_probs = jnp.clip(jnp.exp(math.log(2.0) - 2.0794415 * jax.random.uniform(part_keys[2], (TOKENS, TOPK), jnp.float32) ** level_of(part_keys[2], (TOKENS, TOPK), ((0, 8),), -0.2, 0.2)), 0.25, 2.0)
    expert_ids = draw_expert_ids(jax.random.fold_in(jax.random.fold_in(keys[7], part), 71), part)
    w_gate = bell_draw(keys[4], (EXPERTS, D, FF), D ** -0.5, 0.1875, ((0, 8),))
    w_up = bell_draw(keys[5], (EXPERTS, D, FF), D ** -0.5, 0.1875, ((0, 8),))
    w_down = bell_draw(keys[6], (EXPERTS, FF, D), (FF * D // 64) ** -0.5, 0.0546875, ((0, 8),))
    return {"hidden_in": hidden_in, "out_grad": out_grad, "gate_probs": gate_probs, "expert_ids": expert_ids, "w_gate": w_gate, "w_up": w_up, "w_down": w_down}


def expert_rows(rows_in, rows_grad, gate_w, up_w, down_w):
    gate_pre = jnp.dot(rows_in, gate_w, preferred_element_type=jnp.float32)
    up_pre = jnp.dot(rows_in, up_w, preferred_element_type=jnp.float32)
    sigmoid_a = jax.nn.sigmoid(gate_pre)
    silu_a = gate_pre * sigmoid_a
    hidden = silu_a * up_pre
    hidden_grad = jnp.dot(rows_grad, down_w.T, preferred_element_type=jnp.float32)
    prob_rows = jnp.sum(hidden_grad * hidden, axis=-1).astype(jnp.bfloat16)
    gate_grad = (hidden_grad * up_pre * sigmoid_a * (1.0 + gate_pre * (1.0 - sigmoid_a))).astype(jnp.bfloat16)
    up_grad = (hidden_grad * silu_a).astype(jnp.bfloat16)
    input_rows = jnp.dot(gate_grad, gate_w.T, preferred_element_type=jnp.float32)
    input_rows = input_rows + jnp.dot(up_grad, up_w.T, preferred_element_type=jnp.float32)
    return input_rows.astype(jnp.bfloat16), prob_rows


def reference(hidden_in, out_grad, gate_probs, expert_ids, w_gate, w_up, w_down):
    flat_ids = expert_ids.reshape(-1).astype(jnp.int32)
    total_rows = flat_ids.shape[0]
    capacity = N_EXPERT * MOST
    onehot = (flat_ids[:, None] == jnp.arange(EXPERTS, dtype=jnp.int32)[None, :]).astype(jnp.int32)
    slot_rank = jnp.sum((jnp.cumsum(onehot, axis=0) - 1) * onehot, axis=1).astype(jnp.int32)
    table = jnp.full((EXPERTS, capacity), total_rows, jnp.int32)
    table = table.at[flat_ids, slot_rank].set(jnp.arange(total_rows, dtype=jnp.int32))

    def per_expert(operands):
        gate_w, up_w, down_w, slot_rows = operands
        token_rows = (jnp.minimum(slot_rows, total_rows - 1) // TOPK).astype(jnp.int32)
        return expert_rows(hidden_in[token_rows], out_grad[token_rows], gate_w, up_w, down_w)

    input_rows, prob_rows = lax.map(per_expert, (w_gate, w_up, w_down, table))
    targets = table.reshape(-1)
    row_grads = jnp.zeros((total_rows, D), jnp.bfloat16).at[targets].set(input_rows.reshape(-1, D), mode="drop")
    prob_grads = jnp.zeros((total_rows,), jnp.bfloat16).at[targets].set(prob_rows.reshape(-1), mode="drop")
    weighted = row_grads.reshape(TOKENS, TOPK, D).astype(jnp.float32) * gate_probs[:, :, None]
    input_grad = jnp.sum(weighted, axis=1).astype(jnp.bfloat16)
    return input_grad, prob_grads.reshape(TOKENS, TOPK)
```

```python
import functools
import jax
import jax.numpy as jnp
from jax import lax
from jax.experimental import pallas as pl
from jax.experimental.pallas import tpu as pltpu
from jax.sharding import PartitionSpec as P

EXPERTS = 32
TOPK = 2
MOST = 16
CHUNK = 256


def forward_part(rows_in, gate_w, up_w):
    gate_pre = jnp.einsum("erd,edf->erf", rows_in, gate_w, preferred_element_type=jnp.float32)
    up_pre = jnp.einsum("erd,edf->erf", rows_in, up_w, preferred_element_type=jnp.float32)
    return (gate_pre, up_pre)


def backward_part(gate_pre, up_pre, rows_grad, gate_w, up_w, down_w):
    sigmoid_a = jax.nn.sigmoid(gate_pre)
    silu_a = gate_pre * sigmoid_a
    hidden = silu_a * up_pre
    hidden_grad = jnp.einsum("erd,efd->erf", rows_grad, down_w, preferred_element_type=jnp.float32)
    prob_rows = jnp.sum(hidden_grad * hidden, axis=-1).astype(jnp.bfloat16)
    gate_grad = (hidden_grad * up_pre * sigmoid_a * (1.0 + gate_pre * (1.0 - sigmoid_a))).astype(
        jnp.bfloat16
    )
    up_grad = (hidden_grad * silu_a).astype(jnp.bfloat16)
    input_rows = jnp.einsum("erf,edf->erd", gate_grad, gate_w, preferred_element_type=jnp.float32)
    input_rows = input_rows + jnp.einsum(
        "erf,edf->erd", up_grad, up_w, preferred_element_type=jnp.float32
    )
    return (input_rows.astype(jnp.bfloat16), prob_rows)


def ranks_of(flat_ids, count):
    onehot = (flat_ids[:, None] == jnp.arange(count, dtype=jnp.int32)[None, :]).astype(jnp.int32)
    slot_rank = jnp.sum((jnp.cumsum(onehot, axis=0) - 1) * onehot, axis=1)
    return slot_rank


def exchange_plan(hidden_in, out_grad, gate_probs, expert_ids, w_gate, w_up, w_down):
    width = hidden_in.shape[1]
    tokens_here = hidden_in.shape[0]
    flat_ids = expert_ids.reshape(-1)
    slot_rank = ranks_of(flat_ids, EXPERTS)
    target = flat_ids * MOST + slot_rank
    token_rows = jnp.arange(flat_ids.shape[0], dtype=jnp.int32) // TOPK
    empty = jnp.zeros((EXPERTS * MOST, width), jnp.bfloat16)
    stash_send = empty.at[target].set(hidden_in[token_rows]).reshape(EXPERTS, MOST, width)
    grad_send = empty.at[target].set(out_grad[token_rows]).reshape(EXPERTS, MOST, width)
    stash_recv, grad_recv = (
        lax.all_to_all(stash_send, "expert", split_axis=0, concat_axis=1, tiled=True),
        lax.all_to_all(grad_send, "expert", split_axis=0, concat_axis=1, tiled=True),
    )
    gate_pre, up_pre = forward_part(stash_recv, w_gate, w_up)
    input_rows, prob_rows = backward_part(gate_pre, up_pre, grad_recv, w_gate, w_up, w_down)
    input_back, prob_back = (
        lax.all_to_all(input_rows, "expert", split_axis=1, concat_axis=0, tiled=True),
        lax.all_to_all(prob_rows, "expert", split_axis=1, concat_axis=0, tiled=True),
    )
    picked = input_back.reshape(EXPERTS * MOST, width)[target].reshape(tokens_here, TOPK, width)
    input_grad = jnp.sum(picked.astype(jnp.float32) * gate_probs[:, :, None], axis=1).astype(
        jnp.bfloat16
    )
    prob_grad = prob_back.reshape(-1)[target].reshape(tokens_here, TOPK)
    return (input_grad, prob_grad)


F32, BF16 = jnp.float32, jnp.bfloat16
VMEM = pl.BlockSpec(memory_space=pltpu.VMEM)
SMEM = pl.BlockSpec(memory_space=pltpu.SMEM)
ANY = pl.BlockSpec(memory_space=pl.ANY)


def call(body, outs, operands, flops, scratch=(), left=()):
    specs = [SMEM] + [VMEM] * (len(operands) - 1) + [ANY] * len(left)
    pinned = [operands[0]] + [
        pltpu.with_memory_space_constraint(x, pltpu.VMEM) for x in operands[1:]
    ]
    pinned += [pltpu.with_memory_space_constraint(x, pltpu.HBM) for x in left]
    return pl.pallas_call(
        body,
        out_shape=outs,
        in_specs=specs,
        out_specs=[VMEM] * len(outs),
        scratch_shapes=list(scratch),
        cost_estimate=pl.CostEstimate(flops=flops, bytes_accessed=1 << 20, transcendentals=0),
        compiler_params=pltpu.CompilerParams(vmem_limit_bytes=12 << 20),
    )(*pinned)


def earlier(tokens):
    row = lax.broadcasted_iota(jnp.int32, (tokens, tokens), 0)
    col = lax.broadcasted_iota(jnp.int32, (tokens, tokens), 1)
    return jnp.where(row < col, 1.0, 0.0).astype(BF16)


def ranks_by_lane(mask):
    return jnp.dot(mask.astype(BF16), earlier(mask.shape[1]), preferred_element_type=F32)


def own_tables_body(count, local, me_ref, ids_ref, probs_ref, *refs):
    src_refs, refs = refs[: len(refs) // 2 - 1], refs[len(refs) // 2 - 1 :]
    table_ref, scale_ref, *dst_refs, sem_ref = refs
    copies = [
        pltpu.make_async_copy(src, dst, sem_ref.at[i])
        for i, (src, dst) in enumerate(zip(src_refs, dst_refs))
    ]
    for copy in copies:
        copy.start()
    tokens = ids_ref.shape[1]
    me = me_ref[0]
    expert = lax.broadcasted_iota(jnp.int32, (EXPERTS, tokens), 0)
    hits = [ids_ref[k : k + 1, :] == expert for k in range(TOPK)]
    either = jnp.where(functools.reduce(jnp.logical_or, hits), 1.0, 0.0)
    rank = ranks_by_lane(either)
    place = lax.broadcasted_iota(jnp.int32, (MOST, tokens), 0).astype(F32)
    for k in range(TOPK):
        chosen = ids_ref[k : k + 1, :]
        own_rank = jnp.sum(jnp.where(hits[k], rank, 0.0), axis=0, keepdims=True)
        at_place = jnp.where(own_rank == place, 1.0, 0.0)
        for d in range(count):
            first = lax.bitwise_xor(me, d) * local
            picks = [jnp.where(chosen == first + e, at_place, 0.0) for e in range(local)]
            block = jnp.concatenate(picks, axis=0).T
            table_ref[k * tokens : (k + 1) * tokens, d * local * MOST : (d + 1) * local * MOST] = (
                block.astype(BF16)
            )
        scale_ref[k * tokens : (k + 1) * tokens, :] = jnp.broadcast_to(
            probs_ref[k : k + 1, :], (tokens, tokens)
        ).T
    for copy in copies:
        copy.wait()


def picks_of(local, me, ids):
    tokens = ids.shape[1]
    expert = me * local + lax.broadcasted_iota(jnp.int32, (8, tokens), 0)
    hits = jnp.where(functools.reduce(jnp.logical_or, [ids[k : k + 1, :] == expert for k in range(TOPK)]), 1.0, 0.0)
    rank = ranks_by_lane(hits)
    place = lax.broadcasted_iota(jnp.int32, (MOST, tokens), 0).astype(F32)
    rows = [jnp.where(rank[e : e + 1, :] == place, hits[e : e + 1, :], 0.0) for e in range(local)]
    return jnp.concatenate(rows, axis=0).astype(BF16)


def select_rows(local, d, picks, pieces, dst_ref):
    rows, start = None, 0
    for piece in pieces:
        size = piece.shape[0]
        part = jnp.dot(picks[:, start : start + size], piece[...], preferred_element_type=F32)
        rows = part if rows is None else rows + part
        start += size
    rows = rows.astype(BF16)
    for e in range(local):
        dst_ref[e, d * MOST : (d + 1) * MOST, :] = rows[e * MOST : (e + 1) * MOST, :]


def cut(refs, sizes):
    groups, at = [], 0
    for size in sizes:
        groups.append(refs[at : at + size])
        at += size
    return groups, refs[at:]


def forward_body(sizes, local, me_ref, *refs):
    count = len(sizes)
    ids_refs, refs = refs[:count], refs[count:]
    pieces, refs = cut(refs, sizes)
    gate_ref, up_ref, picks_ref, hidden_ref, silu_ref, slope_ref, rows_ref = refs
    me = me_ref[0]
    for d in range(count):
        picks = picks_of(local, me, ids_refs[d][...])
        picks_ref[d] = picks
        select_rows(local, d, picks, pieces[d], rows_ref)
    width = gate_ref.shape[2]
    for e in range(local):
        for at in range(0, width, CHUNK):
            cols = slice(at, at + CHUNK)
            gate = jnp.dot(rows_ref[e], gate_ref[e, :, cols], preferred_element_type=F32)
            up = jnp.dot(rows_ref[e], up_ref[e, :, cols], preferred_element_type=F32)
            sig = jax.nn.sigmoid(gate)
            silu = gate * sig
            hidden_ref[e, :, cols] = silu * up
            silu_ref[e, :, cols] = silu
            slope_ref[e, :, cols] = up * sig * (1.0 + gate * (1.0 - sig))


NT = (((1,), (1,)), ((), ()))


def backward_body(sizes, local, me_ref, *refs):
    count = len(sizes)
    pieces, refs = cut(refs, sizes)
    gate_ref, up_ref, down_ref, picks_ref, hidden_ref, silu_ref, slope_ref = refs[:7]
    out_refs, prob_refs = refs[7 : 7 + count], refs[7 + count : 7 + 2 * count]
    rows_ref, gate_grad_ref, up_grad_ref = refs[7 + 2 * count :]
    for d in range(count):
        select_rows(local, d, picks_ref[d], pieces[d], rows_ref)
    width, depth = gate_ref.shape[2], gate_ref.shape[1]
    for e in range(local):
        total = None
        for at in range(0, width, CHUNK):
            cols = slice(at, at + CHUNK)
            grad = lax.dot_general(
                rows_ref[e], down_ref[e, cols, :], NT, preferred_element_type=F32
            )
            part = jnp.sum(grad * hidden_ref[e, :, cols], axis=1, keepdims=True)
            total = part if total is None else total + part
            gate_grad_ref[e, :, cols] = (grad * slope_ref[e, :, cols]).astype(BF16)
            up_grad_ref[e, :, cols] = (grad * silu_ref[e, :, cols]).astype(BF16)
        prob = jnp.broadcast_to(total, (total.shape[0], prob_refs[0].shape[1])).astype(BF16)
        for d in range(count):
            prob_refs[d][e * MOST : (e + 1) * MOST, :] = prob[d * MOST : (d + 1) * MOST, :]
        for at in range(0, depth, CHUNK):
            cols = slice(at, at + CHUNK)
            back = lax.dot_general(
                gate_grad_ref[e], gate_ref[e, cols, :], NT, preferred_element_type=F32
            ) + lax.dot_general(up_grad_ref[e], up_ref[e, cols, :], NT, preferred_element_type=F32)
            back = back.astype(BF16)
            for d in range(count):
                out_refs[d][e * MOST : (e + 1) * MOST, cols] = back[d * MOST : (d + 1) * MOST, :]


def combine_body(count, me_ref, *refs):
    rows_refs, prob_refs = refs[:count], refs[count : 2 * count]
    table_ref, scale_ref, out_ref, prob_out_ref = refs[2 * count :]
    tokens, depth = out_ref.shape
    table = table_ref[...]
    prob = jnp.dot(
        table, jnp.concatenate([r[...] for r in prob_refs], axis=0), preferred_element_type=F32
    )
    for k in range(TOPK):
        prob_out_ref[k : k + 1, :] = prob[k * tokens : (k + 1) * tokens, :].T[:1, :].astype(BF16)
    for at in range(0, depth, CHUNK):
        cols = slice(at, at + CHUNK)
        rows = jnp.concatenate([r[:, cols] for r in rows_refs], axis=0)
        picked = jnp.dot(table, rows, preferred_element_type=F32)
        total = None
        for k in range(TOPK):
            span = slice(k * tokens, (k + 1) * tokens)
            scale = jnp.concatenate([scale_ref[span, :]] * (CHUNK // scale_ref.shape[1]), axis=1)
            term = picked[span, :] * scale
            total = term if total is None else total + term
        out_ref[:, cols] = total.astype(BF16)


def shift(x, d, count):
    return lax.ppermute(x, "expert", [(i, i ^ d) for i in range(count)])


def far_pieces(x, count):
    half = x.shape[0] // 2
    a, b = shift(x, 2, count), shift(x, 4, count)
    return a, b, shift(a[:half], 4, count), shift(b[half:], 2, count)


def near_pieces(x, a, b, c0, c1, count):
    own = [[x], [a], [b], [c0, c1]]
    groups = []
    for group in own:
        groups.append(group)
        groups.append([shift(p, 1, count) for p in group])
    return groups


def gather_plan(count, hidden_in, out_grad, gate_probs, expert_ids, w_gate, w_up, w_down):
    tokens, depth = hidden_in.shape
    local, width = w_gate.shape[0], w_gate.shape[2]
    slots = local * MOST
    rows_here = count * MOST
    me = lax.axis_index("expert").astype(jnp.int32).reshape(1)
    ids, probs = expert_ids.T, gate_probs.T

    far_in = far_pieces(hidden_in, count)
    all_ids = [ids] + [shift(ids, d, count) for d in range(1, count)]
    groups_in = near_pieces(hidden_in, *far_in, count)
    held, *_ = lax.optimization_barrier((out_grad, far_in[0], far_in[1]))
    far_grad = far_pieces(held, count)
    groups_grad = near_pieces(out_grad, *far_grad, count)
    sizes = [len(g) for g in groups_in]
    loaded = [hidden_in, out_grad, w_gate, w_up, w_down]
    table, scale, own_in, own_grad, w_gate, w_up, w_down = call(
        functools.partial(own_tables_body, count, local),
        [
            jax.ShapeDtypeStruct((TOPK * tokens, EXPERTS * MOST), BF16),
            jax.ShapeDtypeStruct((TOPK * tokens, tokens), F32),
        ]
        + [pltpu.VMEM(x.shape, x.dtype) for x in loaded],
        [me, ids, probs],
        1 << 20,
        [pltpu.SemaphoreType.DMA((len(loaded),))],
        loaded,
    )
    flat_in = [own_in] + [p for g in groups_in[1:] for p in g]
    flat_grad = [own_grad] + [p for g in groups_grad[1:] for p in g]
    wide = jax.ShapeDtypeStruct((local, rows_here, width), F32)
    picks, hidden, silu, slope = call(
        functools.partial(forward_body, sizes, local),
        [jax.ShapeDtypeStruct((count, slots, tokens), BF16), wide, wide, wide],
        [me, *all_ids, *flat_in, w_gate, w_up],
        4 * local * rows_here * depth * width,
        [pltpu.VMEM((local, rows_here, depth), BF16)],
    )
    outs = call(
        functools.partial(backward_body, sizes, local),
        [jax.ShapeDtypeStruct((slots, depth), BF16)] * count
        + [jax.ShapeDtypeStruct((slots, tokens), BF16)] * count,
        [me, *flat_grad, w_gate, w_up, w_down, picks, hidden, silu, slope],
        6 * local * rows_here * depth * width,
        [pltpu.VMEM((local, rows_here, depth), BF16)]
        + [pltpu.VMEM((local, rows_here, width), BF16)] * 2,
    )
    rows_back = [outs[0]] + [shift(outs[d], d, count) for d in range(1, count)]
    prob_back = [outs[count]] + [shift(outs[count + d], d, count) for d in range(1, count)]
    input_grad, prob_grad = call(
        functools.partial(combine_body, count),
        [
            jax.ShapeDtypeStruct((tokens, depth), BF16),
            jax.ShapeDtypeStruct((TOPK, tokens), BF16),
        ],
        [me, *rows_back, *prob_back, table, scale],
        1 << 28,
    )
    return input_grad, prob_grad.T


def solution(mesh):
    count = mesh.shape["expert"]
    body = functools.partial(gather_plan, count) if count == 8 else exchange_plan
    in_specs = (
        P(("group", "expert"), None),
        P(("group", "expert"), None),
        P(("group", "expert"), None),
        P(("group", "expert"), None),
        P("expert", None, None),
        P("expert", None, None),
        P("expert", None, None),
    )
    out_specs = (P(("group", "expert"), None), P(("group", "expert"), None))
    return jax.shard_map(body, mesh=mesh, in_specs=in_specs, out_specs=out_specs, check_vma=False)
```
